32 devices in a mesh: ga: 2 (over y), aa: 4 (over x, core), ba: 4 (over z).
Axes of the slice: x: 2, y: 2, z: 4, core: 2. Of those that a mesh axis runs over, the one named last changes fastest.
Arguments:
- query: bfloat16 [2048, 5120], P(('ga', 'aa'), 'ba'), parts along dimension 0, may hold values from -64 to 64
- keys: bfloat16 [16384, 1024], P(('ga', 'aa'), 'ba'), parts along dimension 0, may hold values from -16 to 16
- values: bfloat16 [16384, 1024], P(('ga', 'aa'), 'ba'), parts along dimension 0, may hold values from -6 to 6
- cache_lengths: int32 [8], P(('ga', 'aa')), parts along dimension 0, may hold values from 256 to 2048, as said below
- residual: bfloat16 [2048, 5120], P(('ga', 'ba'), 'aa'), parts along dimension 0, may hold values from -16 to 16
- out_weight: bfloat16 [5120, 5120], P('ba', 'aa'), may hold values from -0.078125 to 0.078125
- norm_gain: float32 [5120], P('aa'), may hold values from 0.1 to 1.9
- router_weight: float32 [5120, 4], P('aa'), may hold values from -0.078125 to 0.078125
- expert_ids: int32 [2048], P(('ga', 'ba')), parts along dimension 0, may hold values from 0 to 3
- expert_slots: int32 [2048], P(('ga', 'ba')), parts along dimension 0, may hold values from -1 to 127, as said below
- expert_gate: bfloat16 [4, 5120, 4096], P('ba', None, 'aa'), may hold values from -0.078125 to 0.078125
- expert_up: bfloat16 [4, 5120, 4096], P('ba', None, 'aa'), may hold values from -0.078125 to 0.078125
- expert_down: bfloat16 [4, 4096, 5120], P('ba', 'aa'), may hold values from -0.25 to 0.25
Outputs:
- layer_out: bfloat16 [2048, 5120], P(('ga', 'ba'), 'aa'), parts along dimension 0
The draws below stay inside these ranges and needn't reach their ends.
There are 2 independent parts, one for each index of `ga`. The reference program is written for one: setup_inputs(seed, part) draws one part's arguments, and reference() takes and returns one part's arrays. A program takes and returns all parts, laid end to end along the dimension named above; an argument that names none is the same for every part. Nothing has to cross between parts.
Inputs may be any that keep to these rules, and one draw needn't show every extreme that they name: `cache_lengths`: some shard has 2048 valid positions in every draw. `expert_slots`: rows form aligned blocks of 256 rows (the rows of one index of ba). A row's slot is the number of earlier rows of its block with the same expert id, or -1 where that number is 128 or more. In every draw some expert has all 128 slots filled in every block.
All inputs are finite; a program needn't handle non-finite values.
Results may differ from the reference program's by a relative error of at most 0.019.
Values may be sent and summed in bfloat16 or wider, within the bound.
A program may use at most 128 MiB of HBM per device.

```python
import jax
import jax.numpy as jnp
from jax import lax

D = 5120
H = 40
KVH = 8
HD = 128
FF = 4096
EXP_DEV = 1
Q = 1024
CTX_DEV = 2048
CTX = 8192
EXPERTS = 4
CAPS = 128


def draw_keys(key, part):
    base = jax.random.normal(jax.random.fold_in(key, 3), (CTX, KVH * HD), jnp.float32)
    return jnp.clip(base, -16.0, 16.0).astype(jnp.bfloat16)


def draw_query(key, part):
    base = 3.0 * jax.random.normal(jax.random.fold_in(key, 7), (Q, H * HD), jnp.float32)
    return jnp.clip(base, -64.0, 64.0).astype(jnp.bfloat16)


def draw_residual(key, part):
    columns = jnp.arange(D, dtype=jnp.float32) / D
    base = jax.random.normal(jax.random.fold_in(key, 11), (Q, D), jnp.float32) * (0.4 * 4.0 ** columns)[None, :]
    return jnp.clip(base, -16.0, 16.0).astype(jnp.bfloat16)


def draw_cache_lengths(key, part):
    shards = CTX // CTX_DEV
    lengths = jax.random.randint(jax.random.fold_in(key, 41), (shards,), CTX_DEV // 8, CTX_DEV + 1)
    full = jax.random.randint(jax.random.fold_in(key, 42), (), 0, shards)
    return lengths.at[full].set(CTX_DEV).astype(jnp.int32)


def routing(key):
    base = jax.random.fold_in(key, 29)
    blocks = EXPERTS // EXP_DEV
    rows = Q // blocks
    first = jax.random.randint(jax.random.fold_in(base, 1), (blocks, rows), 0, EXPERTS)
    second = jax.random.randint(jax.random.fold_in(base, 2), (blocks, rows), 0, EXPERTS)
    order = jax.random.permutation(jax.random.fold_in(base, 3), EXPERTS)
    ids = order[jnp.minimum(first, second)]
    scores = jax.random.randint(jax.random.fold_in(base, 4), (blocks, rows), 0, 1 << 20) * rows + jnp.arange(rows, dtype=jnp.int32)[None, :]
    ranks = jnp.argsort(jnp.argsort(scores, axis=1), axis=1)
    ids = jnp.where(ranks < CAPS, order[0], ids)
    onehot = (ids[..., None] == jnp.arange(EXPERTS, dtype=jnp.int32)[None, None, :]).astype(jnp.int32)
    earlier = jnp.sum((jnp.cumsum(onehot, axis=1) - onehot) * onehot, axis=-1)
    slots = jnp.where(earlier < CAPS, earlier, -1)
    return (ids.reshape(Q).astype(jnp.int32), slots.reshape(Q).astype(jnp.int32))


def draw_expert_ids(key, part):
    return routing(key)[0]


def draw_expert_slots(key, part):
    return routing(key)[1]


def block_scale(own_key, shape, pieces, low, high):
    level, own = 1.0, jax.random.fold_in(own_key, 6)
    for axis_at, parts in pieces:
        steps = jnp.exp(jax.random.uniform(jax.random.fold_in(own, axis_at), (parts,), jnp.float32, low / len(pieces), high / len(pieces)))
        level = level * jnp.repeat(steps, shape[axis_at] // parts).reshape([-1 if axis == axis_at else 1 for axis in range(len(shape))])
    return level


def bell_draw(stream_key, extent, width, bound, cuts=(), held_as=jnp.bfloat16):
    entries = jax.random.normal(stream_key, extent, jnp.float32) * width
    if len(cuts) > 0:
        entries = block_scale(stream_key, extent, cuts, -0.22, 0.18) * entries
    return jnp.clip(entries, min=-bound, max=bound).astype(held_as)


def setup_inputs(seed: int = 0, part: int = 0) -> dict:
    splits = jax.random.split(jax.random.key(seed), 14)
    part_splits = jax.random.split(jax.random.fold_in(splits[13], part), 14)
    return {
        "query": draw_query(jax.random.fold_in(jax.random.fold_in(splits[13], part), 71), part),
        "keys": draw_keys(jax.random.fold_in(jax.random.fold_in(splits[13], part), 71), part),
        "values": bell_draw(part_splits[2], (CTX, KVH * HD), 1.0, 6.0, ((0, 4), (1, 4))),
        "cache_lengths": draw_cache_lengths(jax.random.fold_in(jax.random.fold_in(splits[13], part), 71), part),
        "residual": draw_residual(jax.random.fold_in(jax.random.fold_in(splits[13], part), 71), part),
        "out_weight": bell_draw(splits[5], (H * HD, D), (H * HD) ** -0.5, 0.078125, ((0, 4), (1, 4))),
        "norm_gain": jnp.clip(1.0 + 0.18 * jax.random.normal(splits[6], (D,), jnp.float32), 0.1, 1.9),
        "router_weight": bell_draw(splits[7], (D, EXPERTS), D ** -0.5, 0.078125, ((0, 4),), jnp.float32),
        "expert_ids": draw_expert_ids(jax.random.fold_in(jax.random.fold_in(splits[13], part), 71), part),
        "expert_slots": draw_expert_slots(jax.random.fold_in(jax.random.fold_in(splits[13], part), 71), part),
        "expert_gate": bell_draw(splits[10], (EXPERTS, D, FF), D ** -0.5, 0.078125, ((0, 4), (2, 4))),
        "expert_up": bell_draw(splits[11], (EXPERTS, D, FF), D ** -0.5, 0.078125, ((0, 4), (2, 4))),
        "expert_down": bell_draw(splits[12], (EXPERTS, FF, D), (FF // 8) ** -0.5, 0.25, ((0, 4), (1, 4))),
    }


NEGATIVE = -1e+30
EPSILON = 1e-05

def reference(query, keys, values, cache_lengths, residual, out_weight, norm_gain, router_weight, expert_ids, expert_slots, expert_gate, expert_up, expert_down):
    group = H // KVH
    shards = CTX // CTX_DEV
    queries = query.astype(jnp.float32).reshape(Q, KVH, group, HD)

    def one_shard(index):
        start = (index * CTX_DEV).astype(jnp.int32)
        key_block = lax.dynamic_slice_in_dim(keys, start, CTX_DEV, 0).astype(jnp.float32).reshape(CTX_DEV, KVH, HD)
        value_block = lax.dynamic_slice_in_dim(values, start, CTX_DEV, 0).astype(jnp.float32).reshape(CTX_DEV, KVH, HD)
        scores = jnp.einsum('qkgd,tkd->kgqt', queries, key_block) * HD ** (-0.5)
        valid = jnp.arange(CTX_DEV, dtype=jnp.int32) < cache_lengths[index]
        scores = jnp.where(valid, scores, NEGATIVE)
        peak = lax.optimization_barrier(jnp.max(scores, axis=-1))
        probs = jnp.exp(scores - peak[..., None])
        total = lax.optimization_barrier(jnp.sum(probs, axis=-1))
        rounded = lax.optimization_barrier(probs.astype(jnp.bfloat16)).astype(jnp.float32)
        weighted = jnp.einsum('kgqt,tkd->kgqd', rounded, value_block)
        return (peak, total, weighted)
    peaks, totals, outputs = lax.map(one_shard, jnp.arange(shards, dtype=jnp.int32))
    top = lax.optimization_barrier(jnp.max(peaks, axis=0))
    factor = jnp.exp(peaks - top)
    numer = lax.optimization_barrier(jnp.sum(factor[..., None] * outputs, axis=0))
    denom = lax.optimization_barrier(jnp.sum(factor * totals, axis=0))
    attended = (numer / denom[..., None]).transpose(2, 0, 1, 3).reshape(Q, H * HD).astype(jnp.bfloat16)
    hidden = residual.astype(jnp.float32) + jnp.dot(attended, out_weight, preferred_element_type=jnp.float32)
    inverse = 1.0 / jnp.sqrt(lax.optimization_barrier(jnp.mean(hidden * hidden, axis=1)) + EPSILON)
    normed = hidden * inverse[:, None] * norm_gain
    logits = jnp.dot(normed, router_weight, precision=lax.Precision.HIGHEST)
    chosen = expert_ids[:, None] == jnp.arange(EXPERTS, dtype=jnp.int32)[None, :]
    gate = lax.optimization_barrier(jnp.sum(jnp.where(chosen, jax.nn.sigmoid(logits), 0.0), axis=1))
    expert_in = normed.astype(jnp.bfloat16)
    blocks = EXPERTS // EXP_DEV
    rows = Q // blocks
    combined = expert_ids * CAPS + expert_slots
    select = (combined[:, None] == jnp.arange(EXPERTS * CAPS, dtype=jnp.int32)[None, :]) & (expert_slots[:, None] >= 0)
    select = select.astype(jnp.float32).reshape(blocks, rows, EXPERTS, CAPS)
    buffer = jnp.einsum('brec,brd->ebcd', select, expert_in.astype(jnp.float32).reshape(blocks, rows, D))
    buffer = buffer.reshape(EXPERTS, blocks * CAPS, D).astype(jnp.bfloat16)

    def one_expert(operands):
        slots_in, gate_w, up_w, down_w = operands
        gate_part = jnp.dot(slots_in, gate_w, preferred_element_type=jnp.float32)
        up_part = jnp.dot(slots_in, up_w, preferred_element_type=jnp.float32)
        act = (jax.nn.silu(gate_part) * up_part).astype(jnp.bfloat16)
        return jnp.dot(act, down_w, preferred_element_type=jnp.float32).astype(jnp.bfloat16)
    outbuf = lax.map(one_expert, (buffer, expert_gate, expert_up, expert_down))
    outbuf = outbuf.reshape(EXPERTS, blocks, CAPS, D).astype(jnp.float32)
    back = jnp.einsum('brec,ebcd->brd', select, outbuf).reshape(Q, D)
    return (hidden + gate[:, None] * back).astype(jnp.bfloat16)
```

```python
import functools

import jax
import jax.numpy as jnp
from jax import lax
from jax.experimental import pallas as pl
from jax.experimental.pallas import tpu as pltpu
from jax.sharding import PartitionSpec as P

D = 5120
HD = 128
Q = 1024
STEP = 512
LOG2E = 1.4426950408889634


NEGATIVE = -1e30
EPSILON = 1e-05


def attend_kernel(shards, group, lengths, q_ref, *refs):
    key_refs = refs[:shards]
    value_refs = refs[shards : 2 * shards]
    out_ref, stat_ref, peak_ref, total_ref, acc_ref = refs[2 * shards :]
    factor = HD ** (-0.5) * LOG2E
    context = key_refs[0].shape[0]
    step = min(STEP, context)
    peak_ref[...] = jnp.full_like(peak_ref, NEGATIVE)
    total_ref[...] = jnp.zeros_like(total_ref)
    acc_ref[...] = jnp.zeros_like(acc_ref)

    def chunk(shard, start, limit):
        k = key_refs[shard][pl.ds(start, step), :]
        v = value_refs[shard][pl.ds(start, step), :]
        for head in range(group):
            q = q_ref[:, head * HD : (head + 1) * HD]
            scores = lax.dot_general(
                k, q, (((1,), (1,)), ((), ())), preferred_element_type=jnp.float32
            )
            if limit is not None:
                place = lax.broadcasted_iota(jnp.int32, scores.shape, 0)
                scores = jnp.where(place < limit, scores, NEGATIVE)
            old = peak_ref[head : head + 1, :]
            new = jnp.maximum(old, jnp.max(scores, axis=0, keepdims=True))
            probs = jnp.exp2((scores - new) * factor)
            scale = jnp.exp2((old - new) * factor)
            peak_ref[head : head + 1, :] = new
            total_ref[head : head + 1, :] = total_ref[head : head + 1, :] * scale + jnp.sum(
                probs, axis=0, keepdims=True
            )
            acc_ref[head] = acc_ref[head] * scale + lax.dot_general(
                v,
                probs.astype(jnp.bfloat16),
                (((0,), (0,)), ((), ())),
                preferred_element_type=jnp.float32,
            )

    for shard in range(shards):
        length = lengths[shard]
        full = length // step

        @pl.loop(0, full)
        def _(i, shard=shard):
            chunk(shard, pl.multiple_of(i * step, step), None)

        @pl.when(length > full * step)
        def _(shard=shard, full=full, length=length):
            chunk(shard, pl.multiple_of(full * step, step), length - full * step)

    for head in range(group):
        total = total_ref[head : head + 1, :]
        out_ref[:, head * HD : (head + 1) * HD] = jnp.transpose(acc_ref[head] / total).astype(
            out_ref.dtype
        )
    stat_ref[0, 0] = peak_ref[...]
    stat_ref[0, 1] = total_ref[...]


def attend(query, key_blocks, value_blocks, lengths, out_type):
    shards = len(key_blocks)
    rows, width = query.shape
    kv_heads = key_blocks[0].shape[1] // HD
    group = width // HD // kv_heads
    context = key_blocks[0].shape[0]
    kv_spec = pl.BlockSpec((context, HD), lambda g, n: (0, g))
    work = shards * rows * width * context
    return pl.pallas_call(
        functools.partial(attend_kernel, shards, group),
        grid_spec=pltpu.PrefetchScalarGridSpec(
            num_scalar_prefetch=1,
            grid=(kv_heads,),
            in_specs=[pl.BlockSpec((rows, group * HD), lambda g, n: (0, g))]
            + [kv_spec] * (2 * shards),
            out_specs=[
                pl.BlockSpec((rows, group * HD), lambda g, n: (0, g)),
                pl.BlockSpec((1, 2, group, rows), lambda g, n: (g, 0, 0, 0)),
            ],
            scratch_shapes=[
                pltpu.VMEM((group, rows), jnp.float32),
                pltpu.VMEM((group, rows), jnp.float32),
                pltpu.VMEM((group, HD, rows), jnp.float32),
            ],
        ),
        out_shape=[
            jax.ShapeDtypeStruct((rows, width), out_type),
            jax.ShapeDtypeStruct((kv_heads, 2, group, rows), jnp.float32),
        ],
        cost_estimate=pl.CostEstimate(
            flops=8 * work, bytes_accessed=4 * shards * context * kv_heads * HD + 6 * rows * width,
            transcendentals=work // HD,
        ),
        compiler_params=pltpu.CompilerParams(vmem_limit_bytes=32 * 1024 * 1024),
        name="attend",
    )(lengths, query, *key_blocks, *value_blocks)


def span_attention(query, keys, values, cache_lengths):
    size = lax.axis_size("aa")
    swap = [(i, i ^ 1) for i in range(size)]
    far = []
    for hop in range(2, size, 2):
        ahead = [(i, (i + hop) % size) for i in range(size)]
        far.append((lax.ppermute(query, "aa", ahead), [(j, i) for i, j in ahead]))
    near_keys = lax.ppermute(keys, "aa", swap)
    near_values = lax.ppermute(values, "aa", swap)
    near_length = lax.ppermute(cache_lengths, "aa", swap)
    both = jnp.concatenate([cache_lengths, near_length])
    parts = [attend(query, [keys], [values], cache_lengths, jnp.float32)]
    for rows, back in far:
        out, stat = attend(rows, [keys, near_keys], [values, near_values], both, jnp.bfloat16)
        parts.append((lax.ppermute(out, "aa", back), lax.ppermute(stat, "aa", back)))
    parts.append(attend(query, [near_keys], [near_values], near_length, jnp.float32))
    peaks = [stat[:, 0] for _, stat in parts]
    top = functools.reduce(jnp.maximum, peaks)
    weights = [
        stat[:, 1] * jnp.exp((stat[:, 0] - top) * HD ** (-0.5)) for _, stat in parts
    ]
    whole = functools.reduce(jnp.add, weights)
    rows, width = query.shape
    total = 0.0
    for (out, _), weight in zip(parts, weights):
        share = (weight / whole).reshape(width // HD, rows).T
        total = total + out.astype(jnp.float32).reshape(rows, width // HD, HD) * share[:, :, None]
    return total.reshape(rows, width).astype(jnp.bfloat16)


def on_device(
    query,
    keys,
    values,
    cache_lengths,
    residual,
    out_weight,
    norm_gain,
    router_weight,
    expert_ids,
    expert_slots,
    expert_gate,
    expert_up,
    expert_down,
):
    own = span_attention(query, keys, values, cache_lengths)
    attended = lax.all_gather(own, "aa", axis=0, tiled=True)
    hidden = residual.astype(jnp.float32) + lax.psum_scatter(
        jnp.dot(attended, out_weight, preferred_element_type=jnp.float32).astype(jnp.bfloat16),
        "ba",
        scatter_dimension=0,
        tiled=True,
    ).astype(jnp.float32)
    scaled = hidden * norm_gain
    sums = lax.psum(
        jnp.concatenate(
            [
                jnp.dot(scaled, router_weight, precision=lax.Precision.HIGHEST),
                jnp.sum(hidden * hidden, axis=1, keepdims=True),
            ],
            axis=1,
        ),
        "aa",
    )
    inverse = 1.0 / jnp.sqrt(sums[:, -1] / D + EPSILON)
    normed = scaled * inverse[:, None]
    logits = sums[:, :-1] * inverse[:, None]
    experts = router_weight.shape[1]
    chosen = expert_ids[:, None] == lax.broadcasted_iota(jnp.int32, (1, experts), 1)
    gate = jnp.sum(jnp.where(chosen, jax.nn.sigmoid(logits), 0.0), axis=1)
    expert_in = normed.astype(jnp.bfloat16)
    slot_count = 2 * Q // (lax.axis_size("ba") * experts)
    combined = expert_ids * slot_count + expert_slots
    placing = (
        combined[:, None] == lax.broadcasted_iota(jnp.int32, (1, experts * slot_count), 1)
    ) & (expert_slots[:, None] >= 0)
    placing = placing.astype(jnp.bfloat16)
    packed = lax.dot_general(
        placing, expert_in, (((0,), (0,)), ((), ())), preferred_element_type=jnp.float32
    ).astype(jnp.bfloat16)
    arrived = lax.all_to_all(packed, "ba", split_axis=0, concat_axis=0, tiled=True)
    gate_w = expert_gate[0]
    up_w = expert_up[0]
    down_w = expert_down[0]
    piece = lax.all_gather(arrived, "aa", axis=1, tiled=True)
    gate_part = jnp.dot(piece, gate_w, preferred_element_type=jnp.float32)
    up_part = jnp.dot(piece, up_w, preferred_element_type=jnp.float32)
    act = (jax.nn.silu(gate_part) * up_part).astype(jnp.bfloat16)
    expert_out = lax.psum_scatter(
        lax.dot_general(
            down_w, act, (((0,), (1,)), ((), ())), preferred_element_type=jnp.float32
        ).astype(jnp.bfloat16),
        "aa",
        scatter_dimension=0,
        tiled=True,
    )
    returned = lax.all_to_all(expert_out, "ba", split_axis=1, concat_axis=1, tiled=True)
    from_experts = lax.dot_general(
        placing, returned, (((1,), (1,)), ((), ())), preferred_element_type=jnp.float32
    )
    return (hidden + gate[:, None] * from_experts).astype(jnp.bfloat16)


def solution(mesh):
    return jax.shard_map(
        on_device,
        mesh=mesh,
        in_specs=(
            P(("ga", "aa"), "ba"),
            P(("ga", "aa"), "ba"),
            P(("ga", "aa"), "ba"),
            P(("ga", "aa")),
            P(("ga", "ba"), "aa"),
            P("ba", "aa"),
            P("aa"),
            P("aa", None),
            P(("ga", "ba")),
            P(("ga", "ba")),
            P("ba", None, "aa"),
            P("ba", None, "aa"),
            P("ba", "aa", None),
        ),
        out_specs=P(("ga", "ba"), "aa"),
        check_vma=False,
    )
```

```python
import functools

import jax
import jax.numpy as jnp
from jax import lax
from jax.experimental import pallas as pl
from jax.experimental.pallas import tpu as pltpu
from jax.sharding import PartitionSpec as P

D = 5120
HD = 128
Q = 1024
STEP = 512
LANES = 128
LOG2E = 1.4426950408889634


NEGATIVE = -1e30
EPSILON = 1e-05


def attend_kernel(shards, group, lengths, q_ref, *refs):
    key_refs = refs[:shards]
    value_refs = refs[shards : 2 * shards]
    out_ref, stat_ref, peak_ref, total_ref, acc_ref = refs[2 * shards :]
    factor = HD ** (-0.5) * LOG2E
    context = key_refs[0].shape[0]
    step = min(STEP, context)
    peak_ref[...] = jnp.full_like(peak_ref, NEGATIVE)
    total_ref[...] = jnp.zeros_like(total_ref)
    acc_ref[...] = jnp.zeros_like(acc_ref)

    def chunk(shard, start, limit):
        k = key_refs[shard][pl.ds(start, step), :]
        v = value_refs[shard][pl.ds(start, step), :]
        for head in range(group):
            q = q_ref[:, head * HD : (head + 1) * HD]
            scores = lax.dot_general(
                k, q, (((1,), (1,)), ((), ())), preferred_element_type=jnp.float32
            )
            if limit is not None:
                place = lax.broadcasted_iota(jnp.int32, scores.shape, 0)
                scores = jnp.where(place < limit, scores, NEGATIVE)
            old = peak_ref[head : head + 1, :]
            new = jnp.maximum(old, jnp.max(scores, axis=0, keepdims=True))
            probs = jnp.exp2((scores - new) * factor)
            scale = jnp.exp2((old - new) * factor)
            peak_ref[head : head + 1, :] = new
            total_ref[head : head + 1, :] = total_ref[head : head + 1, :] * scale + jnp.sum(
                probs, axis=0, keepdims=True
            )
            acc_ref[head] = acc_ref[head] * scale + lax.dot_general(
                v,
                probs.astype(jnp.bfloat16),
                (((0,), (0,)), ((), ())),
                preferred_element_type=jnp.float32,
            )

    for shard in range(shards):
        length = lengths[shard]
        full = length // step

        @pl.loop(0, full)
        def _(i, shard=shard):
            chunk(shard, pl.multiple_of(i * step, step), None)

        @pl.when(length > full * step)
        def _(shard=shard, full=full, length=length):
            chunk(shard, pl.multiple_of(full * step, step), length - full * step)

    for head in range(group):
        total = total_ref[head : head + 1, :]
        out_ref[:, head * HD : (head + 1) * HD] = jnp.transpose(acc_ref[head] / total).astype(
            out_ref.dtype
        )
    stat_ref[0, 0] = peak_ref[...]
    stat_ref[0, 1] = total_ref[...]


def attend(query, key_blocks, value_blocks, lengths, out_type):
    shards = len(key_blocks)
    rows, width = query.shape
    kv_heads = key_blocks[0].shape[1] // HD
    group = width // HD // kv_heads
    context = key_blocks[0].shape[0]
    kv_spec = pl.BlockSpec((context, HD), lambda g, n: (0, g))
    work = shards * rows * width * context
    return pl.pallas_call(
        functools.partial(attend_kernel, shards, group),
        grid_spec=pltpu.PrefetchScalarGridSpec(
            num_scalar_prefetch=1,
            grid=(kv_heads,),
            in_specs=[pl.BlockSpec((rows, group * HD), lambda g, n: (0, g))]
            + [kv_spec] * (2 * shards),
            out_specs=[
                pl.BlockSpec((rows, group * HD), lambda g, n: (0, g)),
                pl.BlockSpec((1, 2, group, rows), lambda g, n: (g, 0, 0, 0)),
            ],
            scratch_shapes=[
                pltpu.VMEM((group, rows), jnp.float32),
                pltpu.VMEM((group, rows), jnp.float32),
                pltpu.VMEM((group, HD, rows), jnp.float32),
            ],
        ),
        out_shape=[
            jax.ShapeDtypeStruct((rows, width), out_type),
            jax.ShapeDtypeStruct((kv_heads, 2, group, rows), jnp.float32),
        ],
        cost_estimate=pl.CostEstimate(
            flops=8 * work, bytes_accessed=4 * shards * context * kv_heads * HD + 6 * rows * width,
            transcendentals=work // HD,
        ),
        compiler_params=pltpu.CompilerParams(vmem_limit_bytes=32 * 1024 * 1024),
        name="attend",
    )(lengths, query, *key_blocks, *value_blocks)


def span_attention(query, keys, values, cache_lengths):
    size = lax.axis_size("aa")
    swap = [(i, i ^ 1) for i in range(size)]
    far = []
    for hop in range(2, size, 2):
        ahead = [(i, (i + hop) % size) for i in range(size)]
        far.append((lax.ppermute(query, "aa", ahead), [(j, i) for i, j in ahead]))
    near_keys = lax.ppermute(keys, "aa", swap)
    near_values = lax.ppermute(values, "aa", swap)
    near_length = lax.ppermute(cache_lengths, "aa", swap)
    both = jnp.concatenate([cache_lengths, near_length])
    parts = [attend(query, [keys], [values], cache_lengths, jnp.float32)]
    for rows, back in far:
        out, stat = attend(rows, [keys, near_keys], [values, near_values], both, jnp.bfloat16)
        parts.append((lax.ppermute(out, "aa", back), lax.ppermute(stat, "aa", back)))
    parts.append(attend(query, [near_keys], [near_values], near_length, jnp.float32))
    return merge(parts, keys.shape[1] // HD)


def merge_kernel(count, group, *refs):
    stats, outs, out_ref = refs[:count], refs[count : 2 * count], refs[-1]
    factor = HD ** (-0.5) * LOG2E
    rows = out_ref.shape[0]
    top = functools.reduce(jnp.maximum, [stat[0, 0] for stat in stats])
    weights = [stat[0, 1] * jnp.exp2((stat[0, 0] - top) * factor) for stat in stats]
    whole = functools.reduce(jnp.add, weights)
    shares = [weight / whole for weight in weights]
    for head in range(group):
        span = slice(head * HD, (head + 1) * HD)
        terms = [
            out[:, span].astype(jnp.float32)
            * jnp.transpose(jnp.broadcast_to(share[head : head + 1, :], (HD, rows)))
            for out, share in zip(outs, shares)
        ]
        out_ref[:, span] = functools.reduce(jnp.add, terms).astype(out_ref.dtype)


def merge(parts, kv_heads):
    count = len(parts)
    rows, width = parts[0][0].shape
    group = width // HD // kv_heads
    wide = pl.BlockSpec((rows, group * HD), lambda g: (0, g))
    return pl.pallas_call(
        functools.partial(merge_kernel, count, group),
        grid=(kv_heads,),
        in_specs=[pl.BlockSpec((1, 2, group, rows), lambda g: (g, 0, 0, 0))] * count + [wide] * count,
        out_specs=wide,
        out_shape=jax.ShapeDtypeStruct((rows, width), jnp.bfloat16),
        name="merge",
    )(*[stat for _, stat in parts], *[out for out, _ in parts])


def peers_of(me_a, me_b, n, m):
    peers = [{"ba": lax.rem(me_b + k, m)} for k in range(1, m)]
    peers += [{"aa": lax.rem(me_a + hop, n)} for hop in range(2, n, 2)]
    return peers + [{"aa": partner_of(me_a)}]


def partner_of(me_a):
    return me_a + 1 - 2 * lax.rem(me_a, 2)


def meet(peers):
    barrier = pltpu.get_barrier_semaphore()
    for peer in peers:
        pl.semaphore_signal(barrier, inc=1, device_id=peer, device_id_type=pl.DeviceIdType.MESH)
    pl.semaphore_wait(barrier, len(peers))


def remote(source, target, send, receive, peer):
    copy = pltpu.make_async_remote_copy(
        src_ref=source,
        dst_ref=target,
        send_sem=send,
        recv_sem=receive,
        device_id=peer,
        device_id_type=pl.DeviceIdType.MESH,
    )
    copy.start()
    return copy


def dispatch_kernel(n, m, packed, out, own_sem, z_send, z_recv, x_send, x_recv, c_send, c_recv):
    me_a, me_b = lax.axis_index("aa"), lax.axis_index("ba")
    slots, columns = packed.shape[1], packed.shape[2]
    meet(peers_of(me_a, me_b, n, m))

    def place(b, a):
        if len(out.shape) == 3:
            return out.at[a, pl.ds(pl.multiple_of(b * slots, slots), slots)]
        return out.at[
            pl.ds(pl.multiple_of(b * slots, slots), slots),
            pl.ds(pl.multiple_of(a * columns, columns), columns),
        ]

    own = pltpu.make_async_copy(packed.at[me_b], place(me_b, me_a), own_sem)
    own.start()
    over_z = [None]
    for k in range(1, m):
        to = lax.rem(me_b + k, m)
        over_z.append(
            remote(packed.at[to], place(me_b, me_a), z_send.at[k], z_recv.at[k], {"ba": to})
        )
    partner = partner_of(me_a)
    over_x, over_c = {}, {}

    def forward(k):
        b = lax.rem(me_b - k + m, m)
        for j, hop in enumerate(range(2, n, 2), 1):
            over_x[k, j].wait_recv()
            block = place(b, lax.rem(me_a - hop + n, n))
            over_c[k, j] = remote(
                block, block, c_send.at[k, j], c_recv.at[k, j], {"aa": partner}
            )

    for k in range(m):
        if k == 0:
            own.wait()
        else:
            over_z[k].wait_recv()
        block = place(lax.rem(me_b - k + m, m), me_a)
        for j, hop in enumerate(range(2, n, 2), 1):
            over_x[k, j] = remote(
                block,
                block,
                x_send.at[k, j],
                x_recv.at[k, j],
                {"aa": lax.rem(me_a + hop, n)},
            )
        over_c[k, 0] = remote(block, block, c_send.at[k, 0], c_recv.at[k, 0], {"aa": partner})
        if k > 0:
            forward(k - 1)
    forward(m - 1)
    for copy in over_c.values():
        copy.wait_recv()
    for copy in over_z[1:] + list(over_x.values()) + list(over_c.values()):
        copy.wait_send()


def dispatch(packed):
    n, m = lax.axis_size("aa"), lax.axis_size("ba")
    columns = packed.shape[1]
    rows = packed.shape[0] // m
    half = n // 2
    sems = [pltpu.SemaphoreType.DMA((m,))] * 2 + [pltpu.SemaphoreType.DMA((m, half))] * 4
    flat = columns % LANES == 0
    shape = (m * rows, n * columns) if flat else (n, m * rows, columns)
    out = pl.pallas_call(
        functools.partial(dispatch_kernel, n, m),
        out_shape=jax.ShapeDtypeStruct(shape, packed.dtype),
        in_specs=[pl.BlockSpec(memory_space=pltpu.VMEM)],
        out_specs=pl.BlockSpec(memory_space=pltpu.VMEM),
        scratch_shapes=[pltpu.SemaphoreType.DMA] + sems,
        compiler_params=pltpu.CompilerParams(
            collective_id=1, has_side_effects=True, vmem_limit_bytes=24 * 1024 * 1024
        ),
        name="dispatch",
    )(packed.reshape(m, rows, columns))
    return out if flat else out.transpose(1, 0, 2).reshape(m * rows, n * columns)


def combine_kernel(
    n, m, part, out, near, summed, far, total, own_sem, z_send, z_recv, x_send, x_recv, c_send, c_recv
):
    me_a, me_b = lax.axis_index("aa"), lax.axis_index("ba")
    slots, columns = out.shape[1], out.shape[2]
    meet(peers_of(me_a, me_b, n, m))
    partner = partner_of(me_a)

    def piece(k, a):
        b = lax.rem(me_b + k, m)
        if len(part.shape) == 3:
            return part.at[a, pl.ds(pl.multiple_of(b * slots, slots), slots)]
        return part.at[
            pl.ds(pl.multiple_of(b * slots, slots), slots),
            pl.ds(pl.multiple_of(a * columns, columns), columns),
        ]

    order = list(range(1, m)) + [0]
    over_c, over_x = {}, {}
    over_z = [None] * m
    for k in order:
        for j in range(n // 2):
            over_c[k, j] = remote(
                piece(k, lax.rem(partner + 2 * j, n)),
                near.at[k, j],
                c_send.at[k, j],
                c_recv.at[k, j],
                {"aa": partner},
            )

    def join(k, j):
        over_c[k, j].wait_recv()
        mine = piece(k, lax.rem(me_a + 2 * j, n))
        return mine[...].astype(jnp.float32) + near[k, j].astype(jnp.float32)

    def finish(k):
        value = join(k, 0)
        for j in range(1, n // 2):
            over_x[k, j].wait_recv()
            value = value + far[k, j].astype(jnp.float32)
        total[k] = value.astype(total.dtype)
        if k == 0:
            copy = pltpu.make_async_copy(total.at[0], out.at[me_b], own_sem)
            copy.start()
            copy.wait()
        else:
            over_z[k] = remote(
                total.at[k],
                out.at[me_b],
                z_send.at[k],
                z_recv.at[k],
                {"ba": lax.rem(me_b + k, m)},
            )

    for k in order:
        for j in range(1, n // 2):
            summed[k, j] = join(k, j).astype(summed.dtype)
            over_x[k, j] = remote(
                summed.at[k, j],
                far.at[k, j],
                x_send.at[k, j],
                x_recv.at[k, j],
                {"aa": lax.rem(me_a + 2 * j, n)},
            )
    for k in order:
        finish(k)
    for copy in over_z[1:]:
        copy.wait_recv()
    for copy in over_z[1:] + list(over_x.values()) + list(over_c.values()):
        copy.wait_send()


def combine(part):
    n, m = lax.axis_size("aa"), lax.axis_size("ba")
    rows, columns = part.shape[0] // m, part.shape[1] // n
    if columns % LANES:
        part = part.reshape(m * rows, n, columns).transpose(1, 0, 2)
    half = n // 2
    sems = [pltpu.SemaphoreType.DMA((m,))] * 2 + [pltpu.SemaphoreType.DMA((m, half))] * 4
    block = pltpu.VMEM((m, half, rows, columns), part.dtype)
    out = pl.pallas_call(
        functools.partial(combine_kernel, n, m),
        out_shape=jax.ShapeDtypeStruct((m, rows, columns), part.dtype),
        in_specs=[pl.BlockSpec(memory_space=pltpu.VMEM)],
        out_specs=pl.BlockSpec(memory_space=pltpu.VMEM),
        scratch_shapes=[block, block, block, pltpu.VMEM((m, rows, columns), part.dtype)]
        + [pltpu.SemaphoreType.DMA]
        + sems,
        compiler_params=pltpu.CompilerParams(
            collective_id=2, has_side_effects=True, vmem_limit_bytes=40 * 1024 * 1024
        ),
        name="combine",
    )(part)
    return out.reshape(m * rows, columns)


def on_device(
    query,
    keys,
    values,
    cache_lengths,
    residual,
    out_weight,
    norm_gain,
    router_weight,
    expert_ids,
    expert_slots,
    expert_gate,
    expert_up,
    expert_down,
):
    own = span_attention(query, keys, values, cache_lengths)
    attended = lax.all_gather(own, "aa", axis=0, tiled=True)
    hidden = residual.astype(jnp.float32) + lax.psum_scatter(
        jnp.dot(attended, out_weight, preferred_element_type=jnp.float32).astype(jnp.bfloat16),
        "ba",
        scatter_dimension=0,
        tiled=True,
    ).astype(jnp.float32)
    scaled = hidden * norm_gain
    sums = lax.psum(
        jnp.concatenate(
            [
                jnp.dot(scaled, router_weight, precision=lax.Precision.HIGHEST),
                jnp.sum(hidden * hidden, axis=1, keepdims=True),
            ],
            axis=1,
        ),
        "aa",
    )
    inverse = 1.0 / jnp.sqrt(sums[:, -1] / D + EPSILON)
    normed = scaled * inverse[:, None]
    logits = sums[:, :-1] * inverse[:, None]
    experts = router_weight.shape[1]
    chosen = expert_ids[:, None] == lax.broadcasted_iota(jnp.int32, (1, experts), 1)
    gate = jnp.sum(jnp.where(chosen, jax.nn.sigmoid(logits), 0.0), axis=1)
    expert_in = normed.astype(jnp.bfloat16)
    slot_count = 2 * Q // (lax.axis_size("ba") * experts)
    combined = expert_ids * slot_count + expert_slots
    placing = (
        combined[:, None] == lax.broadcasted_iota(jnp.int32, (1, experts * slot_count), 1)
    ) & (expert_slots[:, None] >= 0)
    placing = placing.astype(jnp.bfloat16)
    packed = lax.dot_general(
        placing, expert_in, (((0,), (0,)), ((), ())), preferred_element_type=jnp.float32
    ).astype(jnp.bfloat16)
    piece = dispatch(packed)
    gate_w = expert_gate[0]
    up_w = expert_up[0]
    down_w = expert_down[0]
    gate_part = jnp.dot(piece, gate_w, preferred_element_type=jnp.float32)
    up_part = jnp.dot(piece, up_w, preferred_element_type=jnp.float32)
    act = (jax.nn.silu(gate_part) * up_part).astype(jnp.bfloat16)
    returned = combine(
        jnp.dot(act, down_w, preferred_element_type=jnp.float32).astype(jnp.bfloat16)
    )
    from_experts = jnp.dot(placing, returned, preferred_element_type=jnp.float32)
    return (hidden + gate[:, None] * from_experts).astype(jnp.bfloat16)


def solution(mesh):
    return jax.shard_map(
        on_device,
        mesh=mesh,
        in_specs=(
            P(("ga", "aa"), "ba"),
            P(("ga", "aa"), "ba"),
            P(("ga", "aa"), "ba"),
            P(("ga", "aa")),
            P(("ga", "ba"), "aa"),
            P("ba", "aa"),
            P("aa"),
            P("aa", None),
            P(("ga", "ba")),
            P(("ga", "ba")),
            P("ba", None, "aa"),
            P("ba", None, "aa"),
            P("ba", "aa", None),
        ),
        out_specs=P(("ga", "ba"), "aa"),
        check_vma=False,
    )
```

```python
import functools

import jax
import jax.numpy as jnp
from jax import lax
from jax.experimental import pallas as pl
from jax.experimental.pallas import tpu as pltpu
from jax.sharding import PartitionSpec as P

D = 5120
HD = 128
Q = 1024
STEP = 512
LANES = 128
LOG2E = 1.4426950408889634


NEGATIVE = -1e30
EPSILON = 1e-05


def attend_kernel(shards, group, lengths, q_ref, *refs):
    key_refs = refs[:shards]
    value_refs = refs[shards : 2 * shards]
    out_ref, stat_ref, peak_ref, total_ref, acc_ref = refs[2 * shards :]
    factor = HD ** (-0.5) * LOG2E
    context = key_refs[0].shape[0]
    step = min(STEP, context)
    peak_ref[...] = jnp.full_like(peak_ref, NEGATIVE)
    total_ref[...] = jnp.zeros_like(total_ref)
    acc_ref[...] = jnp.zeros_like(acc_ref)

    def chunk(shard, start, limit):
        k = key_refs[shard][pl.ds(start, step), :]
        v = value_refs[shard][pl.ds(start, step), :]
        for head in range(group):
            q = q_ref[:, head * HD : (head + 1) * HD]
            scores = lax.dot_general(
                k, q, (((1,), (1,)), ((), ())), preferred_element_type=jnp.float32
            )
            if limit is not None:
                place = lax.broadcasted_iota(jnp.int32, scores.shape, 0)
                scores = jnp.where(place < limit, scores, NEGATIVE)
            old = peak_ref[head : head + 1, :]
            new = jnp.maximum(old, jnp.max(scores, axis=0, keepdims=True))
            probs = jnp.exp2((scores - new) * factor)
            scale = jnp.exp2((old - new) * factor)
            peak_ref[head : head + 1, :] = new
            total_ref[head : head + 1, :] = total_ref[head : head + 1, :] * scale + jnp.sum(
                probs, axis=0, keepdims=True
            )
            acc_ref[head] = acc_ref[head] * scale + lax.dot_general(
                v,
                probs.astype(jnp.bfloat16),
                (((0,), (0,)), ((), ())),
                preferred_element_type=jnp.float32,
            )

    for shard in range(shards):
        length = lengths[shard]
        full = length // step

        @pl.loop(0, full)
        def _(i, shard=shard):
            chunk(shard, pl.multiple_of(i * step, step), None)

        @pl.when(length > full * step)
        def _(shard=shard, full=full, length=length):
            chunk(shard, pl.multiple_of(full * step, step), length - full * step)

    for head in range(group):
        total = total_ref[head : head + 1, :]
        out_ref[:, head * HD : (head + 1) * HD] = jnp.transpose(acc_ref[head] / total).astype(
            out_ref.dtype
        )
    stat_ref[0, 0] = peak_ref[...]
    stat_ref[0, 1] = total_ref[...]


def attend(query, key_blocks, value_blocks, lengths, out_type):
    shards = len(key_blocks)
    rows, width = query.shape
    kv_heads = key_blocks[0].shape[1] // HD
    group = width // HD // kv_heads
    context = key_blocks[0].shape[0]
    kv_spec = pl.BlockSpec((context, HD), lambda g, n: (0, g))
    work = shards * rows * width * context
    return pl.pallas_call(
        functools.partial(attend_kernel, shards, group),
        grid_spec=pltpu.PrefetchScalarGridSpec(
            num_scalar_prefetch=1,
            grid=(kv_heads,),
            in_specs=[pl.BlockSpec((rows, group * HD), lambda g, n: (0, g))]
            + [kv_spec] * (2 * shards),
            out_specs=[
                pl.BlockSpec((rows, group * HD), lambda g, n: (0, g)),
                pl.BlockSpec((1, 2, group, rows), lambda g, n: (g, 0, 0, 0)),
            ],
            scratch_shapes=[
                pltpu.VMEM((group, rows), jnp.float32),
                pltpu.VMEM((group, rows), jnp.float32),
                pltpu.VMEM((group, HD, rows), jnp.float32),
            ],
        ),
        out_shape=[
            jax.ShapeDtypeStruct((rows, width), out_type),
            jax.ShapeDtypeStruct((kv_heads, 2, group, rows), jnp.float32),
        ],
        cost_estimate=pl.CostEstimate(
            flops=8 * work, bytes_accessed=4 * shards * context * kv_heads * HD + 6 * rows * width,
            transcendentals=work // HD,
        ),
        compiler_params=pltpu.CompilerParams(vmem_limit_bytes=32 * 1024 * 1024),
        name="attend",
    )(lengths, query, *key_blocks, *value_blocks)


def span_attention(query, keys, values, cache_lengths):
    size = lax.axis_size("aa")
    swap = [(i, i ^ 1) for i in range(size)]
    far = []
    for hop in range(2, size, 2):
        ahead = [(i, (i + hop) % size) for i in range(size)]
        far.append((lax.ppermute(query, "aa", ahead), [(j, i) for i, j in ahead]))
    near_keys = lax.ppermute(keys, "aa", swap)
    near_values = lax.ppermute(values, "aa", swap)
    near_length = lax.ppermute(cache_lengths, "aa", swap)
    both = jnp.concatenate([cache_lengths, near_length])
    parts = [attend(query, [keys], [values], cache_lengths, jnp.float32)]
    for rows, back in far:
        rows, parts[0] = lax.optimization_barrier((rows, parts[0]))
        out, stat = attend(rows, [keys, near_keys], [values, near_values], both, jnp.bfloat16)
        parts.append((lax.ppermute(out, "aa", back), lax.ppermute(stat, "aa", back)))
    parts.append(attend(query, [near_keys], [near_values], near_length, jnp.float32))
    return merge(parts, keys.shape[1] // HD)


def merge_kernel(count, group, *refs):
    stats, outs, out_ref = refs[:count], refs[count : 2 * count], refs[-1]
    factor = HD ** (-0.5) * LOG2E
    rows = out_ref.shape[0]
    top = functools.reduce(jnp.maximum, [stat[0, 0] for stat in stats])
    weights = [stat[0, 1] * jnp.exp2((stat[0, 0] - top) * factor) for stat in stats]
    whole = functools.reduce(jnp.add, weights)
    shares = [weight / whole for weight in weights]
    for head in range(group):
        span = slice(head * HD, (head + 1) * HD)
        terms = [
            out[:, span].astype(jnp.float32)
            * jnp.transpose(jnp.broadcast_to(share[head : head + 1, :], (HD, rows)))
            for out, share in zip(outs, shares)
        ]
        out_ref[:, span] = functools.reduce(jnp.add, terms).astype(out_ref.dtype)


def merge(parts, kv_heads):
    count = len(parts)
    rows, width = parts[0][0].shape
    group = width // HD // kv_heads
    wide = pl.BlockSpec((rows, group * HD), lambda g: (0, g))
    return pl.pallas_call(
        functools.partial(merge_kernel, count, group),
        grid=(kv_heads,),
        in_specs=[pl.BlockSpec((1, 2, group, rows), lambda g: (g, 0, 0, 0))] * count + [wide] * count,
        out_specs=wide,
        out_shape=jax.ShapeDtypeStruct((rows, width), jnp.bfloat16),
        name="merge",
    )(*[stat for _, stat in parts], *[out for out, _ in parts])


def peers_of(me_a, me_b, n, m):
    peers = [{"ba": lax.rem(me_b + k, m)} for k in range(1, m)]
    peers += [{"aa": lax.rem(me_a + hop, n)} for hop in range(2, n, 2)]
    return peers + [{"aa": partner_of(me_a)}]


def partner_of(me_a):
    return me_a + 1 - 2 * lax.rem(me_a, 2)


def meet(peers):
    barrier = pltpu.get_barrier_semaphore()
    for peer in peers:
        pl.semaphore_signal(barrier, inc=1, device_id=peer, device_id_type=pl.DeviceIdType.MESH)
    pl.semaphore_wait(barrier, len(peers))


def remote(source, target, send, receive, peer):
    copy = pltpu.make_async_remote_copy(
        src_ref=source,
        dst_ref=target,
        send_sem=send,
        recv_sem=receive,
        device_id=peer,
        device_id_type=pl.DeviceIdType.MESH,
    )
    copy.start()
    return copy


def dispatch_kernel(local, n, m, packed, out, own_sem, z_send, z_recv, x_send, x_recv, c_send, c_recv):
    me_a, me_b = lax.axis_index("aa"), lax.axis_index("ba")
    slots, columns = packed.shape[1], packed.shape[2]
    meet(peers_of(me_a, me_b, n, 1 if local else m))

    def index(k):
        return k if local else lax.rem(me_b - k + m, m)

    def place(b, a):
        if len(out.shape) == 3:
            return out.at[a, pl.ds(pl.multiple_of(b * slots, slots), slots)]
        return out.at[
            pl.ds(pl.multiple_of(b * slots, slots), slots),
            pl.ds(pl.multiple_of(a * columns, columns), columns),
        ]

    own = []
    for k in range(m if local else 1):
        own.append(pltpu.make_async_copy(packed.at[index(k)], place(index(k), me_a), own_sem.at[k]))
        own[k].start()
    over_z = [None]
    for k in range(1, 1 if local else m):
        to = lax.rem(me_b + k, m)
        over_z.append(
            remote(packed.at[to], place(me_b, me_a), z_send.at[k], z_recv.at[k], {"ba": to})
        )
    partner = partner_of(me_a)
    over_x, over_c = {}, {}

    def forward(k):
        b = index(k)
        for j, hop in enumerate(range(2, n, 2), 1):
            over_x[k, j].wait_recv()
            block = place(b, lax.rem(me_a - hop + n, n))
            over_c[k, j] = remote(
                block, block, c_send.at[k, j], c_recv.at[k, j], {"aa": partner}
            )

    for k in range(m):
        if k < len(own):
            own[k].wait()
        else:
            over_z[k].wait_recv()
        block = place(index(k), me_a)
        for j, hop in enumerate(range(2, n, 2), 1):
            over_x[k, j] = remote(
                block,
                block,
                x_send.at[k, j],
                x_recv.at[k, j],
                {"aa": lax.rem(me_a + hop, n)},
            )
        over_c[k, 0] = remote(block, block, c_send.at[k, 0], c_recv.at[k, 0], {"aa": partner})
        if k > 0:
            forward(k - 1)
    forward(m - 1)
    for copy in over_c.values():
        copy.wait_recv()
    for copy in over_z[1:] + list(over_x.values()) + list(over_c.values()):
        copy.wait_send()


def dispatch(packed, local, m, name, number):
    n = lax.axis_size("aa")
    columns = packed.shape[1]
    rows = packed.shape[0] // m
    half = n // 2
    sems = [pltpu.SemaphoreType.DMA((m,))] * 2 + [pltpu.SemaphoreType.DMA((m, half))] * 4
    flat = columns % LANES == 0 and not local
    shape = (m * rows, n * columns) if flat else (n, m * rows, columns)
    out = pl.pallas_call(
        functools.partial(dispatch_kernel, local, n, m),
        out_shape=jax.ShapeDtypeStruct(shape, packed.dtype),
        in_specs=[pl.BlockSpec(memory_space=pltpu.VMEM)],
        out_specs=pl.BlockSpec(memory_space=pltpu.VMEM),
        scratch_shapes=[pltpu.SemaphoreType.DMA((m,))] + sems,
        compiler_params=pltpu.CompilerParams(
            collective_id=number, has_side_effects=True, vmem_limit_bytes=24 * 1024 * 1024
        ),
        name=name,
    )(packed.reshape(m, rows, columns))
    if local:
        return out.reshape(n * m * rows, columns)
    return out if flat else out.transpose(1, 0, 2).reshape(m * rows, n * columns)


def combine_kernel(
    n, m, part, out, near, summed, far, total, own_sem, z_send, z_recv, x_send, x_recv, c_send, c_recv
):
    me_a, me_b = lax.axis_index("aa"), lax.axis_index("ba")
    slots, columns = out.shape[1], out.shape[2]
    meet(peers_of(me_a, me_b, n, m))
    partner = partner_of(me_a)

    def piece(k, a):
        b = lax.rem(me_b + k, m)
        if len(part.shape) == 3:
            return part.at[a, pl.ds(pl.multiple_of(b * slots, slots), slots)]
        return part.at[
            pl.ds(pl.multiple_of(b * slots, slots), slots),
            pl.ds(pl.multiple_of(a * columns, columns), columns),
        ]

    order = list(range(1, m)) + [0]
    over_c, over_x = {}, {}
    over_z = [None] * m
    for k in order:
        for j in range(n // 2):
            over_c[k, j] = remote(
                piece(k, lax.rem(partner + 2 * j, n)),
                near.at[k, j],
                c_send.at[k, j],
                c_recv.at[k, j],
                {"aa": partner},
            )

    def join(k, j):
        over_c[k, j].wait_recv()
        mine = piece(k, lax.rem(me_a + 2 * j, n))
        return mine[...].astype(jnp.float32) + near[k, j].astype(jnp.float32)

    def finish(k):
        value = join(k, 0)
        for j in range(1, n // 2):
            over_x[k, j].wait_recv()
            value = value + far[k, j].astype(jnp.float32)
        total[k] = value.astype(total.dtype)
        if k == 0:
            copy = pltpu.make_async_copy(total.at[0], out.at[me_b], own_sem)
            copy.start()
            copy.wait()
        else:
            over_z[k] = remote(
                total.at[k],
                out.at[me_b],
                z_send.at[k],
                z_recv.at[k],
                {"ba": lax.rem(me_b + k, m)},
            )

    for k in order:
        for j in range(1, n // 2):
            summed[k, j] = join(k, j).astype(summed.dtype)
            over_x[k, j] = remote(
                summed.at[k, j],
                far.at[k, j],
                x_send.at[k, j],
                x_recv.at[k, j],
                {"aa": lax.rem(me_a + 2 * j, n)},
            )
    for k in order:
        finish(k)
    for copy in over_z[1:]:
        copy.wait_recv()
    for copy in over_z[1:] + list(over_x.values()) + list(over_c.values()):
        copy.wait_send()


def combine(part):
    n, m = lax.axis_size("aa"), lax.axis_size("ba")
    rows, columns = part.shape[0] // m, part.shape[1] // n
    if columns % LANES:
        part = part.reshape(m * rows, n, columns).transpose(1, 0, 2)
    half = n // 2
    sems = [pltpu.SemaphoreType.DMA((m,))] * 2 + [pltpu.SemaphoreType.DMA((m, half))] * 4
    block = pltpu.VMEM((m, half, rows, columns), part.dtype)
    out = pl.pallas_call(
        functools.partial(combine_kernel, n, m),
        out_shape=jax.ShapeDtypeStruct((m, rows, columns), part.dtype),
        in_specs=[pl.BlockSpec(memory_space=pltpu.VMEM)],
        out_specs=pl.BlockSpec(memory_space=pltpu.VMEM),
        scratch_shapes=[block, block, block, pltpu.VMEM((m, rows, columns), part.dtype)]
        + [pltpu.SemaphoreType.DMA]
        + sems,
        compiler_params=pltpu.CompilerParams(
            collective_id=2, has_side_effects=True, vmem_limit_bytes=40 * 1024 * 1024
        ),
        name="combine",
    )(part)
    return out.reshape(m * rows, columns)


def on_device(
    query,
    keys,
    values,
    cache_lengths,
    residual,
    out_weight,
    norm_gain,
    router_weight,
    expert_ids,
    expert_slots,
    expert_gate,
    expert_up,
    expert_down,
):
    own = span_attention(query, keys, values, cache_lengths)
    attended = dispatch(own, True, 4 if own.shape[0] % 64 == 0 else 1, "gather", 3)
    hidden = residual.astype(jnp.float32) + lax.psum_scatter(
        jnp.dot(attended, out_weight, preferred_element_type=jnp.float32).astype(jnp.bfloat16),
        "ba",
        scatter_dimension=0,
        tiled=True,
    ).astype(jnp.float32)
    scaled = hidden * norm_gain
    sums = lax.psum(
        jnp.concatenate(
            [
                jnp.dot(scaled, router_weight, precision=lax.Precision.HIGHEST),
                jnp.sum(hidden * hidden, axis=1, keepdims=True),
            ],
            axis=1,
        ),
        "aa",
    )
    inverse = 1.0 / jnp.sqrt(sums[:, -1] / D + EPSILON)
    normed = scaled * inverse[:, None]
    logits = sums[:, :-1] * inverse[:, None]
    experts = router_weight.shape[1]
    chosen = expert_ids[:, None] == lax.broadcasted_iota(jnp.int32, (1, experts), 1)
    gate = jnp.sum(jnp.where(chosen, jax.nn.sigmoid(logits), 0.0), axis=1)
    expert_in = normed.astype(jnp.bfloat16)
    slot_count = 2 * Q // (lax.axis_size("ba") * experts)
    combined = expert_ids * slot_count + expert_slots
    placing = (
        combined[:, None] == lax.broadcasted_iota(jnp.int32, (1, experts * slot_count), 1)
    ) & (expert_slots[:, None] >= 0)
    placing = placing.astype(jnp.bfloat16)
    packed = lax.dot_general(
        placing, expert_in, (((0,), (0,)), ((), ())), preferred_element_type=jnp.float32
    ).astype(jnp.bfloat16)
    piece = dispatch(packed, False, lax.axis_size("ba"), "dispatch", 1)
    gate_w = expert_gate[0]
    up_w = expert_up[0]
    down_w = expert_down[0]
    gate_part = jnp.dot(piece, gate_w, preferred_element_type=jnp.float32)
    up_part = jnp.dot(piece, up_w, preferred_element_type=jnp.float32)
    act = (jax.nn.silu(gate_part) * up_part).astype(jnp.bfloat16)
    returned = combine(
        jnp.dot(act, down_w, preferred_element_type=jnp.float32).astype(jnp.bfloat16)
    )
    from_experts = jnp.dot(placing, returned, preferred_element_type=jnp.float32)
    return (hidden + gate[:, None] * from_experts).astype(jnp.bfloat16)


def solution(mesh):
    return jax.shard_map(
        on_device,
        mesh=mesh,
        in_specs=(
            P(("ga", "aa"), "ba"),
            P(("ga", "aa"), "ba"),
            P(("ga", "aa"), "ba"),
            P(("ga", "aa")),
            P(("ga", "ba"), "aa"),
            P("ba", "aa"),
            P("aa"),
            P("aa", None),
            P(("ga", "ba")),
            P(("ga", "ba")),
            P("ba", None, "aa"),
            P("ba", None, "aa"),
            P("ba", "aa", None),
        ),
        out_specs=P(("ga", "ba"), "aa"),
        check_vma=False,
    )
```
